32 devices in a mesh: gx: 16 (over z, x, core), gy: 2 (over y).
Axes of the slice: x: 2, y: 2, z: 4, core: 2. Of those that a mesh axis runs over, the one named last changes fastest.
Arguments:
- residual: float32 [4, 3, 16, 128, 512], P(None, None, None, 'gx', 'gy'), may hold values from -6 to 6
- eps_inv: float32 [16, 128, 512], P(None, 'gx', 'gy'), may hold values from 0.08 to 1
- region_ids: int32 [16, 128, 512], P(None, 'gx', 'gy'), may hold values from 0 to 7
- source_mask: int32 [16, 128, 512], P(None, 'gx', 'gy'), may hold values 0 or 1
- pole_a: float32 [8, 2], replicated, may hold values from 1.2 to 1.9602, as said below
- pole_b: float32 [8, 2], replicated, may hold values from -0.98 to -0.8
- pole_c: float32 [8, 2], replicated, may hold values from 0.1 to 0.4
- waveform: float32 [64, 4], replicated, may hold values from -4 to 4
- plan: int32 [4], replicated, may hold values from 0 to 63
Outputs:
- adjoint_e: float32 [4, 3, 16, 128, 512], P(None, None, None, 'gx', 'gy')
- adjoint_h: float32 [4, 3, 16, 128, 512], P(None, None, None, 'gx', 'gy')
The draws below stay inside these ranges and needn't reach their ends.
Inputs may be any that keep to these rules, and one draw needn't show every extreme that they name: For each region and pole, pole_a is at least 1.2 and below 0.99 * (1 - pole_b), so each pole's recurrence is stable.
All inputs are finite; a program needn't handle non-finite values. No bound on the sum of `source_mask` on one device may be relied on, other than what follows from the above.
Results may differ from the reference program's by a relative error of at most 0.00002.
Values sent between devices are 32-bit elements; how exact they have to be, the bound alone decides.
No kernel may reach another device: no remote copies, remote signals or barrier semaphores. Data moves between devices by JAX's collectives and lax.ppermute only.
A program may use at most 64 MiB of HBM per device.

```python
import math
import jax
import jax.numpy as jnp
from jax import lax

NZ = 16
PORTS = 4
STEPS = 4
REGIONS = 8
REC = 64
NX = 128
NY = 512


def pole_pair(key):
    key_b = jax.random.fold_in(key, 101)
    key_a = jax.random.fold_in(key, 202)
    coef_b = jax.random.uniform(key_b, (REGIONS, 2), jnp.float32, -0.98, -0.8)
    share = jax.random.uniform(key_a, (REGIONS, 2), jnp.float32, 0.0, 1.0)
    coef_a = 1.2 + share * (0.99 * (1.0 - coef_b) - 1.2)
    return (coef_a, coef_b)


def draw_pole_a(key, part):
    return pole_pair(key)[0]


def draw_pole_b(key, part):
    return pole_pair(key)[1]


def touch_ends(result, own_key, smallest, high):
    dims = result.shape
    index_at = [jax.random.randint(jax.random.fold_in(own_key, axis), (), 0, dims[axis]) for axis in range(len(dims))]
    result = result.at[tuple(index_at)].set(smallest)
    longest = dims.index(max(dims))
    index_at[longest] = (index_at[longest] + 1) % dims[longest]
    return result.at[tuple(index_at)].set(high)


def block_levels(own_key, extent, split, smallest, top_value):
    factor_of = 1.0
    for position, shards_of in split:
        steps = jax.random.uniform(jax.random.fold_in(jax.random.fold_in(own_key, 6), position), (shards_of,), jnp.float32, smallest / len(split), top_value / len(split))
        factor_of = factor_of * jnp.repeat(jnp.exp(steps), extent[position] // shards_of).reshape((-1,) + (1,) * (len(extent) - 1 - position))
    return factor_of


def centred(key, dims, deviation, limit, shards=(), kind=jnp.bfloat16):
    result = jax.random.normal(key, dims, jnp.float32) * deviation
    if len(shards) > 0:
        result = block_levels(key, dims, shards, -0.22, 0.18) * result
    return jnp.clip(result, min=-limit, max=limit).astype(kind)


def setup_inputs(seed: int = 0) -> dict:
    keys = jax.random.split(jax.random.key(seed), 10)
    residual = centred(keys[0], (PORTS, 3, NZ, NX, NY), 1.0, 6.0, ((3, 16), (4, 2)), jnp.float32)
    eps_inv = jnp.clip(jnp.exp(math.log(1.0) - 2.5257287 * jax.random.uniform(keys[1], (NZ, NX, NY), jnp.float32) ** block_levels(keys[1], (NZ, NX, NY), ((1, 16), (2, 2)), -0.2, 0.2)), 0.08, 1.0)
    region_ids = touch_ends(jax.random.randint(keys[2], (NZ, NX, NY), 0, REGIONS), jax.random.fold_in(keys[2], 1), 0, REGIONS - 1).astype(jnp.int32)
    source_mask = touch_ends((jax.random.randint(keys[3], (NZ, NX, NY), 0, 4) < 1).astype(jnp.int32), jax.random.fold_in(keys[3], 1), 0, 1)
    pole_a = draw_pole_a(jax.random.fold_in(keys[9], 71), 0)
    pole_b = draw_pole_b(jax.random.fold_in(keys[9], 71), 0)
    pole_c = jnp.clip(jax.random.uniform(keys[6], (REGIONS, 2), jnp.float32, 0.1, 0.4), 0.1, 0.4)
    waveform = centred(keys[7], (REC, PORTS), 1.0, 4.0, (), jnp.float32)
    plan = touch_ends(jax.random.randint(keys[8], (STEPS,), 0, REC), jax.random.fold_in(keys[8], 1), 0, REC - 1).astype(jnp.int32)
    return dict(residual=residual, eps_inv=eps_inv, region_ids=region_ids, source_mask=source_mask, pole_a=pole_a, pole_b=pole_b, pole_c=pole_c, waveform=waveform, plan=plan)


def upper_cell(field, axis):
    count = field.shape[axis]
    inner = lax.slice_in_dim(field, 1, count, axis=axis)
    zeros = jnp.zeros_like(lax.slice_in_dim(field, 0, 1, axis=axis))
    return jnp.concatenate([inner, zeros], axis)


def lower_cell(field, axis):
    count = field.shape[axis]
    inner = lax.slice_in_dim(field, 0, count - 1, axis=axis)
    zeros = jnp.zeros_like(lax.slice_in_dim(field, 0, 1, axis=axis))
    return jnp.concatenate([zeros, inner], axis)


def one_port(inputs):
    residual, amplitude, eps_inv, source_mask, coef_list = inputs
    mask_float = source_mask.astype(jnp.float32)
    zeros = jnp.zeros_like(eps_inv)
    elec = [zeros, zeros, zeros]
    magn = [zeros, zeros, zeros]
    state_u = [[zeros, zeros, zeros], [zeros, zeros, zeros]]
    state_v = [[zeros, zeros, zeros], [zeros, zeros, zeros]]
    for index_step in range(STEPS):
        elec = [elec[c] + mask_float * residual[c] * amplitude[index_step] for c in range(3)]
        elec_x, elec_y, elec_z = elec
        curl_x = (upper_cell(elec_z, 2) - elec_z) - (upper_cell(elec_y, 0) - elec_y)
        curl_y = (upper_cell(elec_x, 0) - elec_x) - (upper_cell(elec_z, 1) - elec_z)
        curl_z = (upper_cell(elec_y, 1) - elec_y) - (upper_cell(elec_x, 2) - elec_x)
        magn = [magn[0] - 0.5 * curl_x, magn[1] - 0.5 * curl_y, magn[2] - 0.5 * curl_z]
        magn_x, magn_y, magn_z = magn
        back_x = (magn_z - lower_cell(magn_z, 2)) - (magn_y - lower_cell(magn_y, 0))
        back_y = (magn_x - lower_cell(magn_x, 0)) - (magn_z - lower_cell(magn_z, 1))
        back_z = (magn_y - lower_cell(magn_y, 1)) - (magn_x - lower_cell(magn_x, 2))
        backs = [back_x, back_y, back_z]
        sectioned = [elec[c] + 0.5 * eps_inv * backs[c] for c in range(3)]
        change = [zeros, zeros, zeros]
        for pole in range(2):
            coef_a, coef_b, coef_c = coef_list[pole]
            new_u = [coef_a * state_u[pole][c] + state_v[pole][c] + coef_c * sectioned[c] for c in range(3)]
            state_v[pole] = [coef_b * state_u[pole][c] for c in range(3)]
            change = [change[c] + (new_u[c] - state_u[pole][c]) for c in range(3)]
            state_u[pole] = new_u
        elec = [sectioned[c] - eps_inv * change[c] for c in range(3)]
    return jnp.stack(elec, 0), jnp.stack(magn, 0)


def reference(residual, eps_inv, region_ids, source_mask, pole_a, pole_b, pole_c, waveform, plan):
    coef_list = [(pole_a[region_ids, pole], pole_b[region_ids, pole], pole_c[region_ids, pole]) for pole in range(2)]
    amplitudes = waveform[plan]

    def run_port(port_inputs):
        port_residual, port_amplitude = port_inputs
        return one_port((port_residual, port_amplitude, eps_inv, source_mask, coef_list))

    adjoint_e, adjoint_h = lax.map(run_port, (residual, jnp.transpose(amplitudes)))
    return adjoint_e, adjoint_h
```

```python
import functools

import jax
import jax.numpy as jnp
from jax import lax
from jax.experimental import pallas as pl
from jax.experimental.pallas import tpu as pltpu
from jax.sharding import PartitionSpec as P

LANES = 128
SUB = 8
HALF = LANES // 2
F32 = jnp.float32


def pairs(count, first):
    swaps = []
    for low in range(first, count - 1, 2):
        swaps += [(low, low + 1), (low + 1, low)]
    return swaps


def swap(value, axis, first):
    swaps = pairs(lax.axis_size(axis), first)
    return lax.ppermute(value, axis, swaps) if swaps else jnp.zeros_like(value)


def lane_index():
    return lax.broadcasted_iota(jnp.int32, (1, LANES), 1)


def pack_kernel(res, eps, ids, mask, near, far, strips):
    ports, comps, rows, _ = res.shape
    depth, items, tiles, nz, _ = near.shape
    nx = 2 * depth
    odd = lax.rem(lax.axis_index("gx"), 2)
    lane = lane_index()

    def plane(out, side, j, x):
        def rows_of(t):
            return pl.ds(t * nx + x, nz, stride=tiles * nx)

        masks = [mask[rows_of(t), :].astype(F32) for t in range(tiles)]
        strip = jnp.zeros((nz, LANES), F32)
        for k in range(items):
            vals = []
            for t in range(tiles):
                if k < ports * comps:
                    c, p = divmod(k, ports)
                    v = res[p, c, rows_of(t), :] * masks[t]
                elif k == ports * comps:
                    v = eps[rows_of(t), :]
                else:
                    v = ids[rows_of(t), :].astype(F32)
                out[j, k, t] = v
                vals.append(v)
            edge = jnp.where(lane < 4, vals[0], vals[-1])
            if k:
                edge = pltpu.roll(edge, 8 * k, 1)
            here = ((lane - 8 * k + 4) & (LANES - 1)) < 8
            strip = jnp.where(here, edge, strip)
        strips[side, j] = strip

    def body(j, carry):
        plane(near, 0, j, depth * (1 - odd) + j)
        plane(far, 1, j, depth * odd + j)
        return carry

    lax.fori_loop(0, depth, body, 0)


def solve_kernel(
    near, far, near_got, far_got, strips, strips_near, strips_far, pole_a, pole_b, pole_c, waveform, plan,
    out_e, out_h, elec, magn, hist, src, coef,
):
    depth, items, tiles, nz, _ = near.shape
    ports = waveform.shape[1]
    comps = 3
    regions = pole_a.shape[0]
    nx = 2 * depth
    gx = lax.axis_index("gx")
    gy = lax.axis_index("gy")
    odd = lax.rem(gx, 2)
    lane = lane_index()
    right, left = lane < 4, lane >= LANES - 4
    keep = jnp.where(right | (left & (gy > 0)), 1.0, 0.0).astype(F32)
    base = ports * comps
    amps = [[waveform[plan[s], p] for p in range(ports)] for s in range(depth)]

    gains = []
    for r in range(regions):
        total = [0.0] * depth
        for k in range(2):
            a, b, c = pole_a[r, k], pole_b[r, k], pole_c[r, k]
            before, now = 0.0, c
            for n in range(depth):
                total[n] = total[n] + (now - before)
                before, now = now, a * now + b * before
        gains.append(total)

    def set_coefs(x, t, eps_v, ids_v):
        vals = [jnp.zeros((nz, LANES), F32) for _ in range(depth)]
        for r in range(regions):
            here = ids_v == float(r)
            vals = [jnp.where(here, gains[r][n], vals[n]) for n in range(depth)]
        coef[x, 0, t] = 0.25 * eps_v
        coef[x, 1, t] = 1.0 - eps_v * vals[0]
        for n in range(1, depth):
            coef[x, 1 + n, t] = eps_v * vals[n]

    def take(source, strip, x, j):
        for k in range(items):
            vals = [source[j, k, t] for t in range(tiles)]
            s = strip(j)
            if k:
                s = pltpu.roll(s, LANES - 8 * k, 1)
            vals.append(jnp.where(right | left, s, 0.0))
            if k < base:
                c, p = divmod(k, ports)
                for t in range(tiles + 1):
                    src[x, p, c, t] = vals[t]
                    elec[x, p, c, t, pl.ds(0, nz), :] = amps[0][p] * vals[t]
                    elec[x, p, c, t, pl.ds(nz, SUB), :] = jnp.zeros((SUB, LANES), F32)
                    magn[x, p, c, t, pl.ds(0, SUB), :] = jnp.zeros((SUB, LANES), F32)
            elif k == base:
                eps_vals = vals
            else:
                for t in range(tiles + 1):
                    set_coefs(x, t, eps_vals[t], vals[t])

    def own(side):
        def load(j):
            return strips[side, j]

        return load

    def load_all(j, carry):
        take(near, own(0), depth + depth * (1 - odd) + j, j)
        take(far, own(1), depth + depth * odd + j, j)
        take(near_got, lambda j: strips_near[j], 3 * depth * (1 - odd) + j, j)
        take(far_got, lambda j: strips_far[j], 3 * depth * odd + j, j)
        return carry

    lax.fori_loop(0, depth, load_all, 0)

    def up_y(vals):
        rolled = [pltpu.roll(v, LANES - 1, 1) for v in vals]
        return [jnp.where(lane == LANES - 1, rolled[(t + 1) % (tiles + 1)], rolled[t]) for t in range(tiles + 1)]

    def down_y(vals):
        rolled = [pltpu.roll(v, 1, 1) for v in vals]
        return [jnp.where(lane == 0, rolled[(t - 1) % (tiles + 1)], rolled[t]) for t in range(tiles + 1)]

    everything = range(tiles + 1)

    def step_h(s, x):
        for p in range(ports):
            for z in range(0, nz, SUB):
                def e(c, dx=0, dz=0):
                    return [elec[x + dx, p, c, t, pl.ds(z + dz, SUB), :] for t in everything]

                ex, ey, ez = e(0), e(1), e(2)
                ex_z, ey_z = e(0, 0, 1), e(1, 0, 1)
                ey_x, ez_x = e(1, 1), e(2, 1)
                ex_y, ez_y = up_y(ex), up_y(ez)
                for t in everything:
                    curls = (
                        (ez_y[t] - ez[t]) - (ey_z[t] - ey[t]),
                        (ex_z[t] - ex[t]) - (ez_x[t] - ez[t]),
                        (ey_x[t] - ey[t]) - (ex_y[t] - ex[t]),
                    )
                    for c in range(comps):
                        where = (x, p, c, t, pl.ds(SUB + z, SUB), slice(None))
                        new = -curls[c] if s == 0 else magn[where] - curls[c]
                        magn[where] = new * keep if t == tiles else new

    def step_e(s, x):
        for p in range(ports):
            for z in range(0, nz, SUB):
                def h(c, dx=0, dz=0):
                    return [magn[x + dx, p, c, t, pl.ds(SUB + z + dz, SUB), :] for t in everything]

                hx, hy, hz = h(0), h(1), h(2)
                hx_z, hy_z = h(0, 0, -1), h(1, 0, -1)
                hy_x, hz_x = h(1, -1), h(2, -1)
                hx_y, hz_y = down_y(hx), down_y(hz)
                rows = pl.ds(z, SUB)
                for t in everything:
                    if s == depth - 1 and t == tiles:
                        continue
                    w = [coef[x, n, t, rows, :] for n in range(s + 2)]
                    curls = (
                        (hz[t] - hz_y[t]) - (hy[t] - hy_z[t]),
                        (hx[t] - hx_z[t]) - (hz[t] - hz_x[t]),
                        (hy[t] - hy_x[t]) - (hx[t] - hx_y[t]),
                    )
                    mags = (hx, hy, hz)
                    for c in range(comps):
                        sec = elec[x, p, c, t, rows, :] + w[0] * curls[c]
                        new = w[1] * sec
                        for n in range(1, s + 1):
                            new = new - w[1 + n] * hist[s - n, x, p, c, t, rows, :]
                        if s < depth - 1:
                            hist[s, x, p, c, t, rows, :] = sec
                            elec[x, p, c, t, rows, :] = new + amps[s + 1][p] * src[x, p, c, t, rows, :]
                        else:
                            out = pl.ds(z * tiles * nx + t * nx + (x - depth), SUB, stride=tiles * nx)
                            out_e[p, c, out, :] = new
                            out_h[p, c, out, :] = 0.5 * mags[c][t]

    first = gx == 0

    @pl.when(first)
    def _():
        magn[depth - 1] = jnp.zeros(magn.shape[1:], F32)

    last = 4 * depth - 2
    for s in range(depth):
        low = jnp.where(first, depth, s)
        pl.loop(low, last - s + 1)(functools.partial(step_h, s))
        pl.loop(jnp.where(first, depth, s + 1), last - s + 1)(functools.partial(step_e, s))


def local(residual, eps_inv, region_ids, source_mask, pole_a, pole_b, pole_c, waveform, plan):
    ports, comps, nz, nx, ny = residual.shape
    depth = plan.shape[0]
    tiles = ny // LANES
    assert nx == 2 * depth and ny % LANES == 0 and nx == SUB
    items = ports * comps + 2

    def tiled(v):
        lead = v.shape[:-2]
        v = v.reshape(lead + (nx, tiles, LANES))
        v = jnp.swapaxes(v, -3, -2)
        return v.reshape(lead[:-1] + (nz * tiles * nx, LANES))

    def untiled(v):
        v = v.reshape(v.shape[:-2] + (nz, tiles, nx, LANES))
        v = jnp.swapaxes(v, -3, -2)
        return v.reshape(v.shape[:-2] + (ny,))

    vmem = pl.BlockSpec(memory_space=pltpu.VMEM)
    smem = pl.BlockSpec(memory_space=pltpu.SMEM)
    half = jax.ShapeDtypeStruct((depth, items, tiles, nz, LANES), F32)
    near, far, edges = pl.pallas_call(
        pack_kernel,
        out_shape=(half, half, jax.ShapeDtypeStruct((2, depth, nz, LANES), F32)),
        in_specs=[vmem] * 4,
        out_specs=(vmem,) * 3,
        name="pack",
    )(tiled(residual), tiled(eps_inv), tiled(region_ids), tiled(source_mask))

    far_got = swap(far, "gx", 1)
    near_got = swap(near, "gx", 0)
    one, two = swap(edges, "gy", 0), swap(edges, "gy", 1)
    odd_y = lax.rem(lax.axis_index("gy"), 2) == 1
    lane = lane_index()
    if lax.axis_size("gy") > 2:
        above, below = jnp.where(odd_y, two, one), jnp.where(odd_y, one, two)
    else:
        above, below = jnp.where(odd_y, 0.0, one), jnp.where(odd_y, one, 0.0)
    strips = jnp.where((lane & 7) < 4, above, below)
    strips_near = swap(strips[0], "gx", 0)
    strips_far = swap(strips[1], "gx", 1)

    out = jax.ShapeDtypeStruct((ports, comps, nz * tiles * nx, LANES), F32)
    planes = 2 * nx
    field = (planes, ports, comps, tiles + 1)
    out_e, out_h = pl.pallas_call(
        solve_kernel,
        out_shape=(out, out),
        in_specs=[vmem] * 7 + [smem] * 5,
        out_specs=(vmem, vmem),
        scratch_shapes=[
            pltpu.VMEM(field + (nz + SUB, LANES), F32),
            pltpu.VMEM(field + (nz + SUB, LANES), F32),
            pltpu.VMEM((depth - 1,) + field + (nz, LANES), F32),
            pltpu.VMEM(field + (nz, LANES), F32),
            pltpu.VMEM((planes, 1 + depth, tiles + 1, nz, LANES), F32),
        ],
        compiler_params=pltpu.CompilerParams(vmem_limit_bytes=56 << 20),
        name="solve",
    )(near, far, near_got, far_got, strips, strips_near, strips_far, pole_a, pole_b, pole_c, waveform, plan)
    return untiled(out_e), untiled(out_h)


def solution(mesh):
    placed = (
        P(None, None, None, "gx", "gy"),
        P(None, "gx", "gy"),
        P(None, "gx", "gy"),
        P(None, "gx", "gy"),
        P(),
        P(),
        P(),
        P(),
        P(),
    )
    return jax.shard_map(
        local,
        mesh=mesh,
        in_specs=placed,
        out_specs=(P(None, None, None, "gx", "gy"), P(None, None, None, "gx", "gy")),
        check_vma=False,
    )
```
